32 devices in a mesh: tm: 4 (over x, core), cell: 8 (over z, y).
Axes of the slice: x: 2, y: 2, z: 4, core: 2. Of those that a mesh axis runs over, the one named last changes fastest.
Arguments:
- coords: float32 [4, 64, 4096], P('tm', None, 'cell'), may hold values from -8 to 8
- potentials: float32 [4, 4096], P('tm', 'cell'), may hold values from -6 to 202
Outputs:
- beliefs: float32 [4, 4096], P('tm', 'cell')
The draws below stay inside these ranges and needn't reach their ends.
All inputs are finite; a program needn't handle non-finite values.
Results may differ from the reference program's by a relative error of at most 0.00011.
Values sent between devices are 32-bit elements; how exact they have to be, the bound alone decides.
A program may use at most 64 MiB of HBM per device.

```python
import math
import jax
import jax.numpy as jnp
from jax import lax

DIM = 64
TIMES = 4
CELLS = 4096


def draw_coords(key, part):
    base = jax.random.normal(jax.random.fold_in(key, 71), (TIMES, DIM, CELLS), jnp.float32)
    return jnp.clip(base * 0.25, -8.0, 8.0)


def draw_potentials(key, part):
    own_key = jax.random.fold_in(key, 72)
    return jnp.clip(jax.random.normal(own_key, (TIMES, CELLS), jnp.float32), -6.0, 6.0)


def setup_inputs(seed: int = 0) -> dict:
    arg_keys = jax.random.split(jax.random.key(seed), 3)
    coords = draw_coords(jax.random.fold_in(arg_keys[2], 71), 0)
    potentials = draw_potentials(jax.random.fold_in(arg_keys[2], 71), 0)
    return dict(coords=coords, potentials=potentials)


EPS = 1.0


def message(sources, belief, targets):
    src_sq = jnp.sum(sources * sources, axis=0)
    width = min(512, targets.shape[1])
    blocks = targets.reshape(targets.shape[0], targets.shape[1] // width, width).transpose(1, 0, 2)

    def one_block(block):
        cross = lax.dot_general(sources, block, (((0,), (0,)), ((), ())), precision=lax.Precision.HIGHEST, preferred_element_type=jnp.float32)
        dist = (src_sq[:, None] + jnp.sum(block * block, axis=0)[None, :]) - 2.0 * cross
        score = belief[:, None] - dist / EPS
        return jax.nn.logsumexp(score, axis=0)

    return lax.map(one_block, blocks).reshape(-1)


def reference(coords, potentials):
    offset = math.log(CELLS)
    rows = [potentials[0]]
    for step in range(TIMES - 1):
        result = message(coords[step], rows[-1], coords[step + 1])
        rows.append(result - offset + potentials[step + 1])
    return jnp.stack(rows, axis=0)
```

```python
import functools
import math

import jax
import jax.numpy as jnp
from jax import lax
from jax.experimental import pallas as pl
from jax.experimental.pallas import tpu as pltpu
from jax.sharding import PartitionSpec as P

LOG2E = math.log2(math.e)
LN2 = math.log(2.0)
BATCH = 4
MESH = pl.DeviceIdType.MESH


def xor(a, b, size):
    out, bit = 0, 1
    while bit < size:
        out = out + bit * ((a // bit + b // bit) % 2)
        bit *= 2
    return out


def kernel(
    n,
    coords_hbm,
    pot_hbm,
    out_ref,
    own,
    pot,
    pair,
    pair_pot,
    block,
    rows,
    split_y,
    split_x,
    score,
    x_sq,
    pair_sq,
    top,
    total,
    pout,
    e1,
    parts,
    beliefs,
    final,
    load_sem,
    block_send,
    mirror_send,
    rows_send,
    relay_send,
    pair_send,
    e1_send,
    parts_send,
    final_send,
    block_recv,
    rows_recv,
    pair_recv,
    pair_pot_recv,
    e1_recv,
    parts_recv,
    final_recv,
):
    dim, local = own.shape
    g = n // 2
    offset = math.log(n * local)
    t = lax.axis_index("tm")
    cell = lax.axis_index("cell")
    half = cell // g
    mirror = lax.rem(cell + g, n)
    first_cell = half * g

    def peer(d):
        return first_cell + xor(cell - first_cell, d, g)

    barrier = pltpu.get_barrier_semaphore()

    def greet(group, who):
        pl.semaphore_signal(barrier, inc=1, device_id=(group, who), device_id_type=MESH)

    def remote(src, dst, send, recv, group, who):
        return pltpu.make_async_remote_copy(
            src_ref=src,
            dst_ref=dst,
            send_sem=send,
            recv_sem=recv,
            device_id=(group, who),
            device_id_type=MESH,
        )

    def send_block(d, group):
        return remote(own, block.at[cell], block_send.at[d], block_recv.at[cell], group, peer(d))

    def send_rows(d, group):
        return remote(pot, rows.at[cell], rows_send.at[d], rows_recv.at[cell], group, peer(d))

    def got_block(who):
        return remote(own, block.at[who], block_send.at[0], block_recv.at[who], t, mirror)

    def got_rows(who):
        return remote(pot, rows.at[who], rows_send.at[0], rows_recv.at[who], t, mirror)

    def send_pair(src, slot, index, group, who):
        return remote(src, pair.at[slot], pair_send.at[index], pair_recv.at[slot], group, who)

    def send_pair_pot():
        return remote(pot, pair_pot, mirror_send.at[1], pair_pot_recv, 1, mirror)

    def send_e1(index, group, who):
        return remote(pout, e1.at[half], e1_send.at[index], e1_recv.at[half], group, who)

    def got_e1(slot):
        return remote(pout, e1.at[slot], e1_send.at[0], e1_recv.at[slot], t, mirror)

    def mirror_block():
        return remote(own, block.at[cell], mirror_send.at[0], block_recv.at[cell], 3, mirror)

    def relay(d):
        return remote(
            block.at[mirror], block.at[mirror], relay_send.at[d], block_recv.at[mirror], 3, peer(d)
        )

    def send_parts(d):
        return remote(
            parts.at[cell], parts.at[cell], parts_send.at[d], parts_recv.at[cell], 3, xor(cell, d, n)
        )

    def got_parts(who):
        return remote(parts.at[who], parts.at[who], parts_send.at[0], parts_recv.at[who], 3, mirror)

    def send_final():
        return remote(final, final, final_send, final_recv, 2, cell)

    @pl.when(t == 1)
    def _():
        for d in range(g):
            greet(0, peer(d))
        greet(1, mirror)

    @pl.when(t == 2)
    def _():
        greet(3, cell)

    @pl.when(t == 3)
    def _():
        greet(1, cell)
        greet(1, mirror)
        greet(2, mirror)
        for d in range(g):
            greet(2, peer(d))
        for d in range(1, n):
            greet(3, xor(cell, d, n))

    load_own = pltpu.make_async_copy(coords_hbm.at[0], own, load_sem.at[0])
    load_pot = pltpu.make_async_copy(pot_hbm, pot, load_sem.at[1])
    load_own.start()
    load_pot.start()
    load_own.wait()
    load_pot.wait()
    partners = jnp.where(t == 0, g, jnp.where(t == 1, 3, jnp.where(t == 2, g + 1, n)))
    pl.semaphore_wait(barrier, partners)

    def split(x):
        hi = x.astype(jnp.bfloat16)
        return hi, (x - hi.astype(jnp.float32)).astype(jnp.bfloat16)

    def as_target(slot, x):
        hi, lo = split((x * (2.0 * LOG2E)).T)
        split_y[slot, :, 0:dim] = hi
        split_y[slot, :, dim : 2 * dim] = hi
        split_y[slot, :, 2 * dim : 3 * dim] = lo
        split_y[slot, :, 3 * dim : 4 * dim] = lo

    def as_source(slot, x):
        hi, lo = split(x)
        split_x[slot, pl.ds(0, dim)] = hi
        split_x[slot, pl.ds(dim, dim)] = lo
        split_x[slot, pl.ds(2 * dim, dim)] = hi
        split_x[slot, pl.ds(3 * dim, dim)] = lo

    def square(x):
        return LOG2E * jnp.sum(x * x, axis=0, keepdims=True)

    def make_score(slot, target, source):
        score[slot] = lax.dot_general(
            split_y[target],
            split_x[source],
            (((1,), (0,)), ((), ())),
            preferred_element_type=jnp.float32,
        )

    def tree(op, values):
        while len(values) > 1:
            values = [op(*values[i : i + 2]) if i + 1 < len(values) else values[i] for i in range(0, len(values), 2)]
        return values[0]

    def fold(acc, slots, biases, first):
        size = 32 // len(slots)

        @pl.loop(0, local // size, unroll=8)
        def _(step):
            here = pl.ds(pl.multiple_of(step * size, size), size)
            terms = [
                score[slot, here, pl.ds(k, 128)] + bias[:, k : k + 128]
                for slot, bias in zip(slots, biases)
                for k in range(0, local, 128)
            ]
            new = tree(jnp.maximum, terms)
            if not first:
                old = top[acc, here]
                new = jnp.maximum(old, new)
            mass = tree(jnp.add, [jnp.exp2(term - new) for term in terms])
            if not first:
                mass = mass + total[acc, here] * jnp.exp2(old - new)
            top[acc, here] = new
            total[acc, here] = mass

    def finish(acc):
        tops = top[acc].T
        peak = jnp.max(tops, axis=0, keepdims=True)
        mass = jnp.sum(total[acc].T * jnp.exp2(tops - peak), axis=0, keepdims=True)
        return peak + jnp.log2(mass)

    def join(values):
        peak = tree(jnp.maximum, values)
        return peak + jnp.log2(tree(jnp.add, [jnp.exp2(value - peak) for value in values]))

    @pl.when(t == 0)
    def _():
        for d in range(g):
            send_block(d, 1).start()
            send_rows(d, 1).start()
        out_ref[...] = pot[...]
        for d in range(g):
            send_block(d, 1).wait_send()
            send_rows(d, 1).wait_send()

    @pl.when(t == 1)
    def _():
        to_mirror = send_pair(own, half, 0, 1, mirror)
        to_last = send_pair(own, half, 1, 3, cell)
        pass_on = send_pair(pair.at[1 - half], 1 - half, 2, 3, cell)
        to_mirror.start()
        send_pair_pot().start()
        to_last.start()
        as_target(0, own[...])

        def arrive(d):
            who = peer(d)
            got_block(who).wait_recv()
            got_rows(who).wait_recv()
            x = block[who]
            as_source(d, x)
            x_sq[d] = square(x)

        def step(d, acc, first):
            make_score(acc, acc, d)
            fold(acc, (acc,), (LOG2E * rows[peer(d)] - x_sq[d],), first)

        for d in range(2):
            arrive(d)
            step(d, 0, d == 0)
        send_pair(own, 1 - half, 0, 1, mirror).wait_recv()
        pass_on.start()
        as_target(1, pair[1 - half])
        for d in range(2):
            step(d, 1, d == 0)

        @pl.loop(2, g)
        def _(d):
            arrive(d)
            step(d, 0, False)
            step(d, 1, False)

        pout[half] = finish(0) + LOG2E * (pot[...] - offset) - square(own[...])
        send_pair_pot().wait_recv()
        pout[1 - half] = finish(1) + LOG2E * (pair_pot[...] - offset) - square(pair[1 - half])
        sends = (send_e1(0, 3, mirror), send_e1(1, 3, cell), send_e1(2, 1, mirror))
        for copy in sends:
            copy.start()
        got_e1(1 - half).wait_recv()
        out_ref[...] = LN2 * join([pout[half], e1[1 - half, half]])
        for copy in (to_mirror, to_last, pass_on, send_pair_pot(), *sends):
            copy.wait_send()

    @pl.when(t == 2)
    def _():
        for d in range(g):
            send_block(d, 3).start()
            send_rows(d, 3).start()
            if d == 0:
                mirror_block().start()
        for d in range(g):
            send_block(d, 3).wait_send()
            send_rows(d, 3).wait_send()
        mirror_block().wait_send()
        send_final().wait_recv()
        out_ref[...] = final[...]

    @pl.when(t == 3)
    def _():
        as_target(1, own[...])
        got_block(mirror).wait_recv()
        for d in range(1, g):
            relay(d).start()
        for s in range(2):
            send_pair(own, s, 0, 1, mirror).wait_recv()
            x = pair[s]
            as_source(s, x)
            pair_sq[s] = square(x)

        @pl.loop(0, g)
        def _(d):
            who = peer(d)
            got_block(who).wait_recv()
            got_rows(who).wait_recv()
            x = block[who]
            as_target(0, x)
            x_sq[who] = square(x)
            k = who - first_cell
            for s in range(2):
                make_score(2 * k + s, 0, s)

        for s in range(2):
            got_e1(s).wait_recv()
        biases = [join([e1[0, s], e1[1, s]]) - pair_sq[s] for s in range(2)]

        @pl.loop(0, g)
        def _(k):
            fold(0, (2 * k, 2 * k + 1), biases, True)
            who = first_cell + k
            parts[cell, k] = finish(0) + LOG2E * (rows[who] - offset) - x_sq[who]

        @pl.loop(0, n - 1)
        def _(i):
            send_parts(n - 1 - i).start()

        def prepare(who):
            x = block[who]
            as_source(0, x)
            x_sq[who] = square(x)
            make_score(who, 1, 0)

        @pl.loop(0, g)
        def _(d):
            prepare(peer(d))

        prepare(mirror)

        @pl.loop(1, g)
        def _(d):
            who = lax.rem(peer(d) + g, n)
            got_block(who).wait_recv()
            prepare(who)

        def gather(start, skip):
            @pl.loop(skip, g)
            def _(d):
                who = lax.rem(peer(d) + g, n) if skip == 0 else peer(d)
                got_parts(who).wait_recv()

            @pl.loop(0, g)
            def _(k):
                beliefs[k] = join([parts[start + m, k] for m in range(g)])

            for k in range(0, g, BATCH):
                batch = range(k, min(k + BATCH, g))
                fold(
                    0,
                    [start + m for m in batch],
                    [beliefs[m] - x_sq[start + m] for m in batch],
                    skip == 1 and k == 0,
                )

        gather(first_cell, 1)
        final[...] = LN2 * beliefs[cell - first_cell]
        send_final().start()
        gather(n - g - first_cell, 0)
        out_ref[...] = LN2 * (finish(0) - square(own[...])) - offset + pot[...]

        for d in range(1, g):
            relay(d).wait_send()

        @pl.loop(1, n)
        def _(d):
            send_parts(d).wait_send()

        send_final().wait_send()


def body(n, coords, potentials):
    _, dim, local = coords.shape
    g = n // 2
    f32, bf16 = jnp.float32, jnp.bfloat16
    dma = pltpu.SemaphoreType.DMA
    row = (1, local)
    return pl.pallas_call(
        functools.partial(kernel, n),
        out_shape=pltpu.VMEM((1, local), f32),
        in_specs=[pl.BlockSpec(memory_space=pl.ANY)] * 2,
        out_specs=pl.BlockSpec(memory_space=pltpu.VMEM),
        scratch_shapes=[
            pltpu.VMEM((dim, local), f32),
            pltpu.VMEM(row, f32),
            pltpu.VMEM((2, dim, local), f32),
            pltpu.VMEM(row, f32),
            pltpu.VMEM((n, dim, local), f32),
            pltpu.VMEM((n, *row), f32),
            pltpu.VMEM((2, local, 4 * dim), bf16),
            pltpu.VMEM((g, 4 * dim, local), bf16),
            pltpu.VMEM((n, local, local), f32),
            pltpu.VMEM((n, *row), f32),
            pltpu.VMEM((2, *row), f32),
            pltpu.VMEM((2, local, 128), f32),
            pltpu.VMEM((2, local, 128), f32),
            pltpu.VMEM((2, *row), f32),
            pltpu.VMEM((2, 2, *row), f32),
            pltpu.VMEM((n, g, *row), f32),
            pltpu.VMEM((g, *row), f32),
            pltpu.VMEM(row, f32),
            dma((2,)),
            dma((g,)),
            dma((2,)),
            dma((g,)),
            dma((g,)),
            dma((3,)),
            dma((3,)),
            dma((n,)),
            dma,
            dma((n,)),
            dma((n,)),
            dma((2,)),
            dma,
            dma((2,)),
            dma((n,)),
            dma,
        ],
        compiler_params=pltpu.CompilerParams(
            collective_id=0, has_side_effects=True, vmem_limit_bytes=60 * 1024 * 1024
        ),
        name="sweep",
    )(coords, potentials)


def solution(mesh):
    return jax.shard_map(
        functools.partial(body, mesh.shape["cell"]),
        mesh=mesh,
        in_specs=(P("tm", None, "cell"), P("tm", "cell")),
        out_specs=P("tm", "cell"),
        check_vma=False,
    )
```

```python
import functools
import math

import jax
import jax.numpy as jnp
from jax import lax
from jax.experimental import pallas as pl
from jax.experimental.pallas import tpu as pltpu
from jax.sharding import PartitionSpec as P

LOG2E = math.log2(math.e)
LN2 = math.log(2.0)
BATCH = 4
MESH = pl.DeviceIdType.MESH


def xor(a, b, size):
    out, bit = 0, 1
    while bit < size:
        out = out + bit * ((a // bit + b // bit) % 2)
        bit *= 2
    return out


def kernel(
    n,
    coords_hbm,
    pot_hbm,
    out_ref,
    own,
    pot,
    pair,
    pair_pot,
    block,
    rows,
    split_y,
    split_x,
    score,
    x_sq,
    pair_sq,
    top,
    total,
    pout,
    e1,
    parts,
    beliefs,
    final,
    load_sem,
    block_send,
    mirror_send,
    rows_send,
    relay_send,
    pair_send,
    e1_send,
    parts_send,
    final_send,
    block_recv,
    rows_recv,
    pair_recv,
    pair_pot_recv,
    e1_recv,
    parts_recv,
    final_recv,
):
    dim, local = own.shape
    g = n // 2
    offset = math.log(n * local)
    t = lax.axis_index("tm")
    cell = lax.axis_index("cell")
    half = cell // g
    mirror = lax.rem(cell + g, n)
    first_cell = half * g

    def peer(d):
        return first_cell + xor(cell - first_cell, d, g)

    barrier = pltpu.get_barrier_semaphore()

    def greet(group, who):
        pl.semaphore_signal(barrier, inc=1, device_id=(group, who), device_id_type=MESH)

    def remote(src, dst, send, recv, group, who):
        return pltpu.make_async_remote_copy(
            src_ref=src,
            dst_ref=dst,
            send_sem=send,
            recv_sem=recv,
            device_id=(group, who),
            device_id_type=MESH,
        )

    def send_block(d, group):
        return remote(own, block.at[cell], block_send.at[d], block_recv.at[cell], group, peer(d))

    def send_rows(d, group):
        return remote(pot, rows.at[cell], rows_send.at[d], rows_recv.at[cell], group, peer(d))

    def got_block(who):
        return remote(own, block.at[who], block_send.at[0], block_recv.at[who], t, mirror)

    def got_rows(who):
        return remote(pot, rows.at[who], rows_send.at[0], rows_recv.at[who], t, mirror)

    def send_pair(src, slot, index, group, who):
        return remote(src, pair.at[slot], pair_send.at[index], pair_recv.at[slot], group, who)

    def send_pair_pot():
        return remote(pot, pair_pot, mirror_send.at[1], pair_pot_recv, 1, mirror)

    def send_e1(index, group, who):
        return remote(pout, e1.at[half], e1_send.at[index], e1_recv.at[half], group, who)

    def got_e1(slot):
        return remote(pout, e1.at[slot], e1_send.at[0], e1_recv.at[slot], t, mirror)

    def mirror_block():
        return remote(own, block.at[cell], mirror_send.at[0], block_recv.at[cell], 3, mirror)

    def relay(d):
        return remote(
            block.at[mirror], block.at[mirror], relay_send.at[d], block_recv.at[mirror], 3, peer(d)
        )

    def send_parts(d):
        return remote(
            parts.at[cell], parts.at[cell], parts_send.at[d], parts_recv.at[cell], 3, xor(cell, d, n)
        )

    def got_parts(who):
        return remote(parts.at[who], parts.at[who], parts_send.at[0], parts_recv.at[who], 3, mirror)

    def send_final():
        return remote(final, final, final_send, final_recv, 2, cell)

    @pl.when(t == 1)
    def _():
        for d in range(g):
            greet(0, peer(d))
        greet(1, mirror)

    @pl.when(t == 2)
    def _():
        greet(3, cell)

    @pl.when(t == 3)
    def _():
        greet(1, cell)
        greet(1, mirror)
        greet(2, mirror)
        for d in range(g):
            greet(2, peer(d))
        for d in range(1, n):
            greet(3, xor(cell, d, n))

    load_own = pltpu.make_async_copy(coords_hbm.at[0], own, load_sem.at[0])
    load_pot = pltpu.make_async_copy(pot_hbm, pot, load_sem.at[1])
    load_own.start()
    load_pot.start()
    load_own.wait()
    load_pot.wait()
    partners = jnp.where(t == 0, g, jnp.where(t == 1, 3, jnp.where(t == 2, g + 1, n)))
    pl.semaphore_wait(barrier, partners)

    def split(x):
        hi = x.astype(jnp.bfloat16)
        return hi, (x - hi.astype(jnp.float32)).astype(jnp.bfloat16)

    def as_target(slot, x):
        hi, lo = split((x * (2.0 * LOG2E)).T)
        split_y[slot, :, 0:dim] = hi
        split_y[slot, :, dim : 2 * dim] = hi
        split_y[slot, :, 2 * dim : 3 * dim] = lo
        split_y[slot, :, 3 * dim : 4 * dim] = lo

    def as_source(slot, x):
        hi, lo = split(x)
        split_x[slot, pl.ds(0, dim)] = hi
        split_x[slot, pl.ds(dim, dim)] = lo
        split_x[slot, pl.ds(2 * dim, dim)] = hi
        split_x[slot, pl.ds(3 * dim, dim)] = lo

    def square(x):
        return LOG2E * jnp.sum(x * x, axis=0, keepdims=True)

    def make_score(slot, target, source):
        score[slot] = lax.dot_general(
            split_y[target],
            split_x[source],
            (((1,), (0,)), ((), ())),
            preferred_element_type=jnp.float32,
        )

    def tree(op, values):
        while len(values) > 1:
            values = [op(*values[i : i + 2]) if i + 1 < len(values) else values[i] for i in range(0, len(values), 2)]
        return values[0]

    def fold(acc, slots, biases, first):
        size = 32 if len(slots) == 1 else 8
        for start in range(0, local, size):
            here = pl.ds(start, size)
            terms = [
                score[slot, here, pl.ds(k, 128)] + bias[:, k : k + 128]
                for slot, bias in zip(slots, biases)
                for k in range(0, local, 128)
            ]
            new = tree(jnp.maximum, terms)
            if not first:
                old = top[acc, here]
                new = jnp.maximum(old, new)
            mass = tree(jnp.add, [jnp.exp2(term - new) for term in terms])
            if not first:
                mass = mass + total[acc, here] * jnp.exp2(old - new)
            top[acc, here] = new
            total[acc, here] = mass

    def finish(acc):
        tops = top[acc].T
        peak = jnp.max(tops, axis=0, keepdims=True)
        mass = jnp.sum(total[acc].T * jnp.exp2(tops - peak), axis=0, keepdims=True)
        return peak + jnp.log2(mass)

    def join(values):
        peak = tree(jnp.maximum, values)
        return peak + jnp.log2(tree(jnp.add, [jnp.exp2(value - peak) for value in values]))

    @pl.when(t == 0)
    def _():
        for d in range(g):
            send_block(d, 1).start()
            send_rows(d, 1).start()
        out_ref[...] = pot[...]
        for d in range(g):
            send_block(d, 1).wait_send()
            send_rows(d, 1).wait_send()

    @pl.when(t == 1)
    def _():
        to_mirror = send_pair(own, half, 0, 1, mirror)
        to_last = send_pair(own, half, 1, 3, cell)
        pass_on = send_pair(pair.at[1 - half], 1 - half, 2, 3, cell)
        to_mirror.start()
        send_pair_pot().start()
        to_last.start()
        as_target(0, own[...])

        def arrive(d):
            who = peer(d)
            got_block(who).wait_recv()
            got_rows(who).wait_recv()
            x = block[who]
            as_source(d, x)
            x_sq[d] = square(x)

        def bias(d):
            return LOG2E * rows[peer(d)] - x_sq[d]

        for d in range(2):
            arrive(d)
            make_score(d, 0, d)
            fold(0, (d,), (bias(d),), d == 0)
        send_pair(own, 1 - half, 0, 1, mirror).wait_recv()
        pass_on.start()
        as_target(1, pair[1 - half])
        for d in range(2):
            make_score(2 + d, 1, d)
        fold(1, (2, 3), (bias(0), bias(1)), True)

        @pl.loop(2, g)
        def _(d):
            arrive(d)
            for acc in range(2):
                make_score(acc, acc, d)
            for acc in range(2):
                fold(acc, (acc,), (bias(d),), False)

        pout[half] = finish(0) + LOG2E * (pot[...] - offset) - square(own[...])
        send_pair_pot().wait_recv()
        pout[1 - half] = finish(1) + LOG2E * (pair_pot[...] - offset) - square(pair[1 - half])
        sends = (send_e1(0, 3, mirror), send_e1(1, 3, cell), send_e1(2, 1, mirror))
        for copy in sends:
            copy.start()
        got_e1(1 - half).wait_recv()
        out_ref[...] = LN2 * join([pout[half], e1[1 - half, half]])
        for copy in (to_mirror, to_last, pass_on, send_pair_pot(), *sends):
            copy.wait_send()

    @pl.when(t == 2)
    def _():
        for d in range(g):
            send_block(d, 3).start()
            send_rows(d, 3).start()
            if d == 0:
                mirror_block().start()
        for d in range(g):
            send_block(d, 3).wait_send()
            send_rows(d, 3).wait_send()
        mirror_block().wait_send()
        send_final().wait_recv()
        out_ref[...] = final[...]

    @pl.when(t == 3)
    def _():
        as_target(g, own[...])

        def arrive_pair(slot):
            send_pair(own, slot, 0, 1, mirror).wait_recv()
            x = pair[slot]
            as_source(slot, x)
            pair_sq[slot] = square(x)

        arrive_pair(half)

        @pl.loop(0, g)
        def _(d):
            who = peer(d)
            got_block(who).wait_recv()
            got_rows(who).wait_recv()
            x = block[who]
            k = who - first_cell
            as_target(k, x)
            x_sq[who] = square(x)
            make_score(2 * k + half, k, half)

        got_block(mirror).wait_recv()
        for d in range(1, g):
            relay(d).start()
        arrive_pair(1 - half)

        @pl.loop(0, g)
        def _(k):
            make_score(2 * k + 1 - half, k, 1 - half)

        for s in range(2):
            got_e1(s).wait_recv()
        biases = [join([e1[0, s], e1[1, s]]) - pair_sq[s] for s in range(2)]

        @pl.loop(0, g // 2)
        def _(i):
            for acc in range(2):
                k = 2 * i + acc
                fold(acc, (2 * k, 2 * k + 1), biases, True)
            for acc in range(2):
                k = 2 * i + acc
                who = first_cell + k
                parts[cell, k] = finish(acc) + LOG2E * (rows[who] - offset) - x_sq[who]

        @pl.loop(0, n - 1)
        def _(i):
            send_parts(n - 1 - i).start()

        def prepare(who):
            x = block[who]
            as_source(0, x)
            x_sq[who] = square(x)
            make_score(who, g, 0)

        @pl.loop(0, g)
        def _(d):
            prepare(peer(d))

        prepare(mirror)

        @pl.loop(1, g)
        def _(d):
            who = lax.rem(peer(d) + g, n)
            got_block(who).wait_recv()
            prepare(who)

        def gather(start, skip):
            @pl.loop(skip, g)
            def _(d):
                who = lax.rem(peer(d) + g, n) if skip == 0 else peer(d)
                got_parts(who).wait_recv()

            @pl.loop(0, g)
            def _(k):
                beliefs[k] = join([parts[start + m, k] for m in range(g)])

            def fold_batch(first, size, begin):
                batch = [first + i for i in range(size)]
                fold(
                    0,
                    [start + m for m in batch],
                    [beliefs[m] - x_sq[start + m] for m in batch],
                    begin,
                )

            fold_batch(0, min(BATCH, g), skip == 1)

            @pl.loop(1, g // BATCH)
            def _(i):
                fold_batch(i * BATCH, BATCH, False)

        gather(first_cell, 1)
        final[...] = LN2 * beliefs[cell - first_cell]
        send_final().start()
        gather(n - g - first_cell, 0)
        out_ref[...] = LN2 * (finish(0) - square(own[...])) - offset + pot[...]

        for d in range(1, g):
            relay(d).wait_send()

        @pl.loop(1, n)
        def _(d):
            send_parts(d).wait_send()

        send_final().wait_send()


def body(n, coords, potentials):
    _, dim, local = coords.shape
    g = n // 2
    f32, bf16 = jnp.float32, jnp.bfloat16
    dma = pltpu.SemaphoreType.DMA
    row = (1, local)
    return pl.pallas_call(
        functools.partial(kernel, n),
        out_shape=pltpu.VMEM((1, local), f32),
        in_specs=[pl.BlockSpec(memory_space=pl.ANY)] * 2,
        out_specs=pl.BlockSpec(memory_space=pltpu.VMEM),
        scratch_shapes=[
            pltpu.VMEM((dim, local), f32),
            pltpu.VMEM(row, f32),
            pltpu.VMEM((2, dim, local), f32),
            pltpu.VMEM(row, f32),
            pltpu.VMEM((n, dim, local), f32),
            pltpu.VMEM((n, *row), f32),
            pltpu.VMEM((g + 1, local, 4 * dim), bf16),
            pltpu.VMEM((g, 4 * dim, local), bf16),
            pltpu.VMEM((n, local, local), f32),
            pltpu.VMEM((n, *row), f32),
            pltpu.VMEM((2, *row), f32),
            pltpu.VMEM((2, local, 128), f32),
            pltpu.VMEM((2, local, 128), f32),
            pltpu.VMEM((2, *row), f32),
            pltpu.VMEM((2, 2, *row), f32),
            pltpu.VMEM((n, g, *row), f32),
            pltpu.VMEM((g, *row), f32),
            pltpu.VMEM(row, f32),
            dma((2,)),
            dma((g,)),
            dma((2,)),
            dma((g,)),
            dma((g,)),
            dma((3,)),
            dma((3,)),
            dma((n,)),
            dma,
            dma((n,)),
            dma((n,)),
            dma((2,)),
            dma,
            dma((2,)),
            dma((n,)),
            dma,
        ],
        compiler_params=pltpu.CompilerParams(
            collective_id=0, has_side_effects=True, vmem_limit_bytes=60 * 1024 * 1024
        ),
        name="sweep",
    )(coords, potentials)


def solution(mesh):
    return jax.shard_map(
        functools.partial(body, mesh.shape["cell"]),
        mesh=mesh,
        in_specs=(P("tm", None, "cell"), P("tm", "cell")),
        out_specs=P("tm", "cell"),
        check_vma=False,
    )
```

```python
import functools
import math

import jax
import jax.numpy as jnp
from jax import lax
from jax.experimental import pallas as pl
from jax.experimental.pallas import tpu as pltpu
from jax.sharding import PartitionSpec as P

LOG2E = math.log2(math.e)
LN2 = math.log(2.0)
BATCH = 4
MESH = pl.DeviceIdType.MESH


def xor(a, b, size):
    out, bit = 0, 1
    while bit < size:
        out = out + bit * ((a // bit + b // bit) % 2)
        bit *= 2
    return out


def kernel(
    n,
    coords_hbm,
    pot_hbm,
    out_ref,
    own,
    pot,
    pair,
    pair_pot,
    block,
    rows,
    split_y,
    split_x,
    score,
    x_sq,
    pair_sq,
    top,
    total,
    pout,
    e1,
    parts,
    beliefs,
    final,
    load_sem,
    block_send,
    early_send,
    mirror_send,
    rows_send,
    relay_send,
    pair_send,
    e1_send,
    parts_send,
    final_send,
    block_recv,
    rows_recv,
    pair_recv,
    pair_pot_recv,
    e1_recv,
    parts_recv,
    final_recv,
    ready,
):
    dim, local = own.shape
    g = n // 2
    h = g // 2
    offset = math.log(n * local)
    t = lax.axis_index("tm")
    cell = lax.axis_index("cell")
    half = cell // g
    mirror = lax.rem(cell + g, n)
    first_cell = half * g

    def peer(d):
        return first_cell + xor(cell - first_cell, d, g)

    barrier = pltpu.get_barrier_semaphore()

    def greet(group, who):
        pl.semaphore_signal(barrier, inc=1, device_id=(group, who), device_id_type=MESH)

    def remote(src, dst, send, recv, group, who):
        return pltpu.make_async_remote_copy(
            src_ref=src,
            dst_ref=dst,
            send_sem=send,
            recv_sem=recv,
            device_id=(group, who),
            device_id_type=MESH,
        )

    def send_block(d, group):
        return remote(own, block.at[cell], block_send.at[d], block_recv.at[cell], group, peer(d))

    def send_rows(d, group):
        return remote(pot, rows.at[cell], rows_send.at[d], rows_recv.at[cell], group, peer(d))

    def got_block(who):
        return remote(own, block.at[who], block_send.at[0], block_recv.at[who], t, mirror)

    def got_rows(who):
        return remote(pot, rows.at[who], rows_send.at[0], rows_recv.at[who], t, mirror)

    def send_pair(src, slot, index, group, who):
        return remote(src, pair.at[slot], pair_send.at[index], pair_recv.at[slot], group, who)

    def send_pair_pot():
        return remote(pot, pair_pot, mirror_send.at[1], pair_pot_recv, 1, mirror)

    def send_e1(index, group, who):
        return remote(pout, e1.at[half], e1_send.at[index], e1_recv.at[half], group, who)

    def got_e1(slot):
        return remote(pout, e1.at[slot], e1_send.at[0], e1_recv.at[slot], t, mirror)

    def mirror_block():
        return remote(own, block.at[cell], mirror_send.at[0], block_recv.at[cell], 3, mirror)

    def relay(d):
        return remote(
            block.at[mirror], block.at[mirror], relay_send.at[d], block_recv.at[mirror], 3, peer(d)
        )

    def parts_copy(side, owner, d, who):
        ref = parts.at[owner, pl.ds(side * h, g - h if side else h)]
        return remote(ref, ref, parts_send.at[d], parts_recv.at[side, owner], 3, who)

    def send_parts(side, d):
        return parts_copy(side, cell, d, xor(cell, d, n))

    def got_parts(side, owner):
        return parts_copy(side, owner, 0, mirror)

    def send_early(d):
        return remote(own, block.at[mirror], early_send.at[d], block_recv.at[mirror], 1, peer(d))

    def send_rows_early(d):
        return remote(pot, rows.at[mirror], rows_send.at[d], rows_recv.at[mirror], 1, peer(d))

    def send_final():
        return remote(final, final, final_send, final_recv, 2, cell)

    @pl.when(t == 1)
    def _():
        for d in range(g):
            greet(0, peer(d))
        greet(1, mirror)
        for d in range(h):
            greet(2, peer(d))
        for d in range(n):
            greet(3, xor(cell, d, n))

    @pl.when(t == 2)
    def _():
        greet(3, cell)

    @pl.when(t == 3)
    def _():
        greet(1, cell)
        greet(2, mirror)
        for d in range(g):
            greet(2, peer(d))
        for d in range(1, n):
            greet(3, xor(cell, d, n))

    load_own = pltpu.make_async_copy(coords_hbm.at[0], own, load_sem.at[0])
    load_pot = pltpu.make_async_copy(pot_hbm, pot, load_sem.at[1])
    load_own.start()
    load_pot.start()
    load_own.wait()
    load_pot.wait()
    partners = jnp.where(t == 0, g, jnp.where(t == 1, 2, jnp.where(t == 2, g + 1 + h, 2 * n)))
    pl.semaphore_wait(barrier, partners)

    def split(x):
        hi = x.astype(jnp.bfloat16)
        return hi, (x - hi.astype(jnp.float32)).astype(jnp.bfloat16)

    def as_target(slot, x):
        hi, lo = split((x * (2.0 * LOG2E)).T)
        split_y[slot, :, 0:dim] = hi
        split_y[slot, :, dim : 2 * dim] = hi
        split_y[slot, :, 2 * dim : 3 * dim] = lo
        split_y[slot, :, 3 * dim : 4 * dim] = lo

    def as_source(slot, x):
        hi, lo = split(x)
        split_x[slot, pl.ds(0, dim)] = hi
        split_x[slot, pl.ds(dim, dim)] = lo
        split_x[slot, pl.ds(2 * dim, dim)] = hi
        split_x[slot, pl.ds(3 * dim, dim)] = lo

    def square(x):
        return LOG2E * jnp.sum(x * x, axis=0, keepdims=True)

    def make_score(slot, target, source):
        score[slot] = lax.dot_general(
            split_y[target],
            split_x[source],
            (((1,), (0,)), ((), ())),
            preferred_element_type=jnp.float32,
        )

    def tree(op, values):
        while len(values) > 1:
            values = [op(*values[i : i + 2]) if i + 1 < len(values) else values[i] for i in range(0, len(values), 2)]
        return values[0]

    def fold(acc, slots, biases, first):
        size = 32 if len(slots) == 1 else 8
        for start in range(0, local, size):
            here = pl.ds(start, size)
            terms = [
                score[slot, here, pl.ds(k, 128)] + bias[:, k : k + 128]
                for slot, bias in zip(slots, biases)
                for k in range(0, local, 128)
            ]
            new = tree(jnp.maximum, terms)
            if not first:
                old = top[acc, here]
                new = jnp.maximum(old, new)
            mass = tree(jnp.add, [jnp.exp2(term - new) for term in terms])
            if not first:
                mass = mass + total[acc, here] * jnp.exp2(old - new)
            top[acc, here] = new
            total[acc, here] = mass

    def finish(acc):
        tops = top[acc].T
        peak = jnp.max(tops, axis=0, keepdims=True)
        mass = jnp.sum(total[acc].T * jnp.exp2(tops - peak), axis=0, keepdims=True)
        return peak + jnp.log2(mass)

    def join(values):
        peak = tree(jnp.maximum, values)
        return peak + jnp.log2(tree(jnp.add, [jnp.exp2(value - peak) for value in values]))

    def message(begin, end, biases):
        @pl.loop(begin // 2, end // 2)
        def _(i):
            for acc in range(2):
                d = 2 * i + acc
                fold(acc, (2 * d, 2 * d + 1), biases, True)
            for acc in range(2):
                d = 2 * i + acc
                who = lax.rem(peer(d) + g, n) if begin == 0 else peer(d)
                square_of = x_sq[d] if begin == 0 else x_sq[who]
                parts[cell, d] = finish(acc) + LOG2E * (rows[who] - offset) - square_of

    @pl.when(t == 0)
    def _():
        for d in range(g):
            send_block(d, 1).start()
            send_rows(d, 1).start()
        out_ref[...] = pot[...]
        for d in range(g):
            send_block(d, 1).wait_send()
            send_rows(d, 1).wait_send()

    @pl.when(t == 1)
    def _():
        to_mirror = send_pair(own, half, 0, 1, mirror)
        to_last = send_pair(own, half, 1, 3, cell)
        pass_on = send_pair(pair.at[1 - half], 1 - half, 2, 3, cell)
        to_mirror.start()
        send_pair_pot().start()
        to_last.start()
        as_target(0, own[...])

        def arrive(d):
            who = peer(d)
            got_block(who).wait_recv()
            got_rows(who).wait_recv()
            x = block[who]
            as_source(d, x)
            x_sq[d] = square(x)

        def bias(d):
            return LOG2E * rows[peer(d)] - x_sq[d]

        for d in range(2):
            arrive(d)
            make_score(d, 0, d)
            fold(0, (d,), (bias(d),), d == 0)
        send_pair(own, 1 - half, 0, 1, mirror).wait_recv()
        pass_on.start()
        as_target(1, pair[1 - half])
        for d in range(2):
            make_score(2 + d, 1, d)
        fold(1, (2, 3), (bias(0), bias(1)), True)

        @pl.loop(2, g)
        def _(d):
            arrive(d)
            for acc in range(2):
                make_score(acc, acc, d)
            for acc in range(2):
                fold(acc, (acc,), (bias(d),), False)

        pout[half] = finish(0) + LOG2E * (pot[...] - offset) - square(own[...])
        send_pair_pot().wait_recv()
        pout[1 - half] = finish(1) + LOG2E * (pair_pot[...] - offset) - square(pair[1 - half])
        pl.semaphore_wait(ready, n)
        sends = (send_e1(0, 3, mirror), send_e1(1, 1, mirror), send_e1(2, 3, cell))
        for copy in sends:
            copy.start()

        for slot, x in ((half, own[...]), (1 - half, pair[1 - half])):
            as_source(slot, x)
            pair_sq[slot] = square(x)

        for d in range(h):
            who = lax.rem(peer(d) + g, n)
            got_block(who).wait_recv()
            got_rows(who).wait_recv()
            x = block[who]
            as_target(d, x)
            x_sq[d] = square(x)
            for s in range(2):
                make_score(2 * d + s, d, s)

        got_e1(1 - half).wait_recv()
        joined = [join([pout[s], e1[1 - half, s]]) for s in range(2)]
        message(0, h, [joined[s] - pair_sq[s] for s in range(2)])

        @pl.loop(0, n)
        def _(i):
            send_parts(0, n - 1 - i).start()

        out_ref[...] = LN2 * join([pout[half], e1[1 - half, half]])
        for copy in (to_mirror, to_last, pass_on, send_pair_pot(), *sends):
            copy.wait_send()

        @pl.loop(0, n)
        def _(d):
            send_parts(0, d).wait_send()

    @pl.when(t == 2)
    def _():
        for d in range(g):
            if d < h:
                send_early(d).start()
                send_rows_early(d).start()
            else:
                send_rows(d, 3).start()
            send_block(d, 3).start()
            if d == 0:
                mirror_block().start()
        for d in range(g):
            if d < h:
                send_early(d).wait_send()
                send_rows_early(d).wait_send()
            else:
                send_rows(d, 3).wait_send()
            send_block(d, 3).wait_send()
        mirror_block().wait_send()
        send_final().wait_recv()
        out_ref[...] = final[...]

    @pl.when(t == 3)
    def _():
        for d in range(n):
            pl.semaphore_signal(ready, inc=1, device_id=(1, xor(cell, d, n)), device_id_type=MESH)
        as_target(g, own[...])

        def arrive_pair(slot):
            send_pair(own, slot, 0, 1, mirror).wait_recv()
            x = pair[slot]
            as_source(slot, x)
            pair_sq[slot] = square(x)

        arrive_pair(half)

        @pl.loop(h, g)
        def _(d):
            who = peer(d)
            got_block(who).wait_recv()
            got_rows(who).wait_recv()
            x = block[who]
            as_target(d, x)
            x_sq[who] = square(x)
            make_score(2 * d + half, d, half)

        got_block(mirror).wait_recv()
        for d in range(1, g):
            relay(d).start()
        arrive_pair(1 - half)

        @pl.loop(h, g)
        def _(d):
            make_score(2 * d + 1 - half, d, 1 - half)

        for s in range(2):
            got_e1(s).wait_recv()
        biases = [join([e1[0, s], e1[1, s]]) - pair_sq[s] for s in range(2)]

        message(h, g, biases)

        @pl.loop(0, n - 1)
        def _(i):
            send_parts(1, n - 1 - i).start()

        def prepare(who):
            x = block[who]
            as_source(0, x)
            x_sq[who] = square(x)
            make_score(who, g, 0)

        @pl.loop(0, h)
        def _(d):
            got_block(peer(d)).wait_recv()
            prepare(peer(d))

        @pl.loop(h, g)
        def _(d):
            prepare(peer(d))

        prepare(mirror)

        @pl.loop(1, g)
        def _(d):
            who = lax.rem(peer(d) + g, n)
            got_block(who).wait_recv()
            prepare(who)

        def gather(start, skip):
            @pl.loop(0, g)
            def _(m):
                got_parts(0, start + m).wait_recv()

            @pl.loop(skip, g)
            def _(d):
                who = lax.rem(peer(d) + g, n) if skip == 0 else peer(d)
                got_parts(1, who).wait_recv()

            @pl.loop(0, g, unroll=BATCH)
            def _(k):
                beliefs[k] = join([parts[start + m, xor(k, m, g)] for m in range(g)])

            def fold_batch(first, size, begin):
                batch = [first + i for i in range(size)]
                fold(
                    0,
                    [start + m for m in batch],
                    [beliefs[m] - x_sq[start + m] for m in batch],
                    begin,
                )

            fold_batch(0, min(BATCH, g), skip == 1)

            @pl.loop(1, g // BATCH)
            def _(i):
                fold_batch(i * BATCH, BATCH, False)

        gather(first_cell, 1)
        final[...] = LN2 * beliefs[cell - first_cell]
        send_final().start()
        gather(n - g - first_cell, 0)
        out_ref[...] = LN2 * (finish(0) - square(own[...])) - offset + pot[...]

        for d in range(1, g):
            relay(d).wait_send()

        @pl.loop(1, n)
        def _(d):
            send_parts(1, d).wait_send()

        send_final().wait_send()


def body(n, coords, potentials):
    _, dim, local = coords.shape
    g = n // 2
    f32, bf16 = jnp.float32, jnp.bfloat16
    dma = pltpu.SemaphoreType.DMA
    row = (1, local)
    return pl.pallas_call(
        functools.partial(kernel, n),
        out_shape=pltpu.VMEM((1, local), f32),
        in_specs=[pl.BlockSpec(memory_space=pl.ANY)] * 2,
        out_specs=pl.BlockSpec(memory_space=pltpu.VMEM),
        scratch_shapes=[
            pltpu.VMEM((dim, local), f32),
            pltpu.VMEM(row, f32),
            pltpu.VMEM((2, dim, local), f32),
            pltpu.VMEM(row, f32),
            pltpu.VMEM((n, dim, local), f32),
            pltpu.VMEM((n, *row), f32),
            pltpu.VMEM((g + 1, local, 4 * dim), bf16),
            pltpu.VMEM((g, 4 * dim, local), bf16),
            pltpu.VMEM((n, local, local), f32),
            pltpu.VMEM((n, *row), f32),
            pltpu.VMEM((2, *row), f32),
            pltpu.VMEM((2, local, 128), f32),
            pltpu.VMEM((2, local, 128), f32),
            pltpu.VMEM((2, *row), f32),
            pltpu.VMEM((2, 2, *row), f32),
            pltpu.VMEM((n, g, *row), f32),
            pltpu.VMEM((g, *row), f32),
            pltpu.VMEM(row, f32),
            dma((2,)),
            dma((g,)),
            dma((g // 2,)),
            dma((2,)),
            dma((g,)),
            dma((g,)),
            dma((3,)),
            dma((3,)),
            dma((n,)),
            dma,
            dma((n,)),
            dma((n,)),
            dma((2,)),
            dma,
            dma((2,)),
            dma((2, n)),
            dma,
            pltpu.SemaphoreType.REGULAR,
        ],
        compiler_params=pltpu.CompilerParams(
            collective_id=0, has_side_effects=True, vmem_limit_bytes=60 * 1024 * 1024
        ),
        name="sweep",
    )(coords, potentials)


def solution(mesh):
    return jax.shard_map(
        functools.partial(body, mesh.shape["cell"]),
        mesh=mesh,
        in_specs=(P("tm", None, "cell"), P("tm", "cell")),
        out_specs=P("tm", "cell"),
        check_vma=False,
    )
```

```python
import functools
import math

import jax
import jax.numpy as jnp
from jax import lax
from jax.experimental import pallas as pl
from jax.experimental.pallas import tpu as pltpu
from jax.sharding import PartitionSpec as P

LOG2E = math.log2(math.e)
LN2 = math.log(2.0)
BATCH = 4
MESH = pl.DeviceIdType.MESH


def xor(a, b, size):
    out, bit = 0, 1
    while bit < size:
        out = out + bit * ((a // bit + b // bit) % 2)
        bit *= 2
    return out


def kernel(
    n,
    coords_hbm,
    pot_hbm,
    out_ref,
    own,
    pot,
    pair,
    pair_pot,
    block,
    rows,
    split_y,
    split_x,
    score,
    x_sq,
    pair_sq,
    top,
    total,
    pout,
    e1,
    parts,
    beliefs,
    final,
    load_sem,
    block_send,
    chunk_send,
    early_send,
    mirror_send,
    rows_send,
    relay_send,
    pair_send,
    e1_send,
    parts_send,
    final_send,
    block_recv,
    chunk_recv,
    rows_recv,
    pair_recv,
    pair_pot_recv,
    e1_recv,
    parts_recv,
    final_recv,
    ready,
):
    dim, local = own.shape
    g = n // 2
    h = g // 2
    offset = math.log(n * local)
    t = lax.axis_index("tm")
    cell = lax.axis_index("cell")
    half = cell // g
    mirror = lax.rem(cell + g, n)
    first_cell = half * g

    def peer(d):
        return first_cell + xor(cell - first_cell, d, g)

    direct = [*range(2, g, 2), 1, 0]

    barrier = pltpu.get_barrier_semaphore()

    def greet(group, who):
        pl.semaphore_signal(barrier, inc=1, device_id=(group, who), device_id_type=MESH)

    def remote(src, dst, send, recv, group, who):
        return pltpu.make_async_remote_copy(
            src_ref=src,
            dst_ref=dst,
            send_sem=send,
            recv_sem=recv,
            device_id=(group, who),
            device_id_type=MESH,
        )

    def send_chunk(d, chunk):
        part = pl.ds(chunk * (dim // 2), dim // 2)
        return remote(
            own.at[part], block.at[cell, part], chunk_send.at[d, chunk], chunk_recv.at[cell, chunk], 1, peer(d)
        )

    def pass_chunk(d, chunk):
        ref = block.at[peer(d), pl.ds(chunk * (dim // 2), dim // 2)]
        return remote(ref, ref, chunk_send.at[d, chunk], chunk_recv.at[peer(d), chunk], 1, peer(1))

    def pass_rows(d):
        ref = rows.at[peer(d)]
        return remote(ref, ref, rows_send.at[d], rows_recv.at[peer(d)], 1, peer(1))

    def send_block(d, group):
        return remote(own, block.at[cell], block_send.at[d], block_recv.at[cell], group, peer(d))

    def send_rows(d, group):
        return remote(pot, rows.at[cell], rows_send.at[d], rows_recv.at[cell], group, peer(d))

    def got_block(who):
        return remote(own, block.at[who], block_send.at[0], block_recv.at[who], t, mirror)

    def got_rows(who):
        return remote(pot, rows.at[who], rows_send.at[0], rows_recv.at[who], t, mirror)

    def send_pair(src, slot, index, group, who):
        return remote(src, pair.at[slot], pair_send.at[index], pair_recv.at[slot], group, who)

    def send_pair_pot():
        return remote(pot, pair_pot, mirror_send.at[1], pair_pot_recv, 1, mirror)

    def send_e1(index, group, who):
        return remote(pout, e1.at[half], e1_send.at[index], e1_recv.at[half], group, who)

    def got_e1(slot):
        return remote(pout, e1.at[slot], e1_send.at[0], e1_recv.at[slot], t, mirror)

    def mirror_block():
        return remote(own, block.at[cell], mirror_send.at[0], block_recv.at[cell], 3, mirror)

    def relay(d):
        return remote(
            block.at[mirror], block.at[mirror], relay_send.at[d], block_recv.at[mirror], 3, peer(d)
        )

    def parts_copy(side, owner, d, who):
        ref = parts.at[owner, pl.ds(side * h, g - h if side else h)]
        return remote(ref, ref, parts_send.at[d], parts_recv.at[side, owner], 3, who)

    def send_parts(side, d):
        return parts_copy(side, cell, d, xor(cell, d, n))

    def got_parts(side, owner):
        return parts_copy(side, owner, 0, mirror)

    def send_early(d):
        return remote(own, block.at[mirror], early_send.at[d], block_recv.at[mirror], 1, peer(d))

    def send_rows_early(d):
        return remote(pot, rows.at[mirror], rows_send.at[d], rows_recv.at[mirror], 1, peer(d))

    def send_final():
        return remote(final, final, final_send, final_recv, 2, cell)

    @pl.when(t == 1)
    def _():
        for d in direct:
            greet(0, peer(d))
        greet(1, peer(1))
        greet(1, mirror)
        for d in range(h):
            greet(2, peer(d))
        for d in range(n):
            greet(3, xor(cell, d, n))

    @pl.when(t == 2)
    def _():
        greet(3, cell)

    @pl.when(t == 3)
    def _():
        greet(1, cell)
        greet(2, mirror)
        for d in range(g):
            greet(2, peer(d))
        for d in range(1, n):
            greet(3, xor(cell, d, n))

    load_own = pltpu.make_async_copy(coords_hbm.at[0], own, load_sem.at[0])
    load_pot = pltpu.make_async_copy(pot_hbm, pot, load_sem.at[1])
    load_own.start()
    load_pot.start()
    load_own.wait()
    load_pot.wait()
    partners = jnp.where(t == 0, len(direct), jnp.where(t == 1, 3, jnp.where(t == 2, g + 1 + h, 2 * n)))
    pl.semaphore_wait(barrier, partners)

    def split(x):
        hi = x.astype(jnp.bfloat16)
        return hi, (x - hi.astype(jnp.float32)).astype(jnp.bfloat16)

    def as_target(slot, x):
        hi, lo = split((x * (2.0 * LOG2E)).T)
        split_y[slot, :, 0:dim] = hi
        split_y[slot, :, dim : 2 * dim] = hi
        split_y[slot, :, 2 * dim : 3 * dim] = lo
        split_y[slot, :, 3 * dim : 4 * dim] = lo

    def as_source(slot, x):
        hi, lo = split(x)
        split_x[slot, pl.ds(0, dim)] = hi
        split_x[slot, pl.ds(dim, dim)] = lo
        split_x[slot, pl.ds(2 * dim, dim)] = hi
        split_x[slot, pl.ds(3 * dim, dim)] = lo

    def square(x):
        return LOG2E * jnp.sum(x * x, axis=0, keepdims=True)

    def make_score(slot, target, source):
        score[slot] = lax.dot_general(
            split_y[target],
            split_x[source],
            (((1,), (0,)), ((), ())),
            preferred_element_type=jnp.float32,
        )

    def tree(op, values):
        while len(values) > 1:
            values = [op(*values[i : i + 2]) if i + 1 < len(values) else values[i] for i in range(0, len(values), 2)]
        return values[0]

    def fold(acc, slots, biases, first):
        size = 32 if len(slots) == 1 else 8
        for start in range(0, local, size):
            here = pl.ds(start, size)
            terms = [
                score[slot, here, pl.ds(k, 128)] + bias[:, k : k + 128]
                for slot, bias in zip(slots, biases)
                for k in range(0, local, 128)
            ]
            new = tree(jnp.maximum, terms)
            if not first:
                old = top[acc, here]
                new = jnp.maximum(old, new)
            mass = tree(jnp.add, [jnp.exp2(term - new) for term in terms])
            if not first:
                mass = mass + total[acc, here] * jnp.exp2(old - new)
            top[acc, here] = new
            total[acc, here] = mass

    def finish(acc):
        tops = top[acc].T
        peak = jnp.max(tops, axis=0, keepdims=True)
        mass = jnp.sum(total[acc].T * jnp.exp2(tops - peak), axis=0, keepdims=True)
        return peak + jnp.log2(mass)

    def join(values):
        peak = tree(jnp.maximum, values)
        return peak + jnp.log2(tree(jnp.add, [jnp.exp2(value - peak) for value in values]))

    def message(begin, end, biases):
        @pl.loop(begin // 2, end // 2)
        def _(i):
            for acc in range(2):
                d = 2 * i + acc
                fold(acc, (2 * d, 2 * d + 1), biases, True)
            for acc in range(2):
                d = 2 * i + acc
                who = lax.rem(peer(d) + g, n) if begin == 0 else peer(d)
                square_of = x_sq[d] if begin == 0 else x_sq[who]
                parts[cell, d] = finish(acc) + LOG2E * (rows[who] - offset) - square_of

    @pl.when(t == 0)
    def _():
        for d in direct:
            send_chunk(d, 0).start()
            send_rows(d, 1).start()
            send_chunk(d, 1).start()
        out_ref[...] = pot[...]
        for d in direct:
            for chunk in range(2):
                send_chunk(d, chunk).wait_send()
            send_rows(d, 1).wait_send()

    @pl.when(t == 1)
    def _():
        to_mirror = send_pair(own, half, 0, 1, mirror)
        to_last = send_pair(own, half, 1, 3, cell)
        pass_on = send_pair(pair.at[1 - half], 1 - half, 2, 3, cell)
        to_last.start()
        as_target(0, own[...])

        def got_chunk(d, chunk):
            return pass_chunk(d, chunk).wait_recv()

        def use(d):
            x = block[peer(d)]
            as_source(d, x)
            x_sq[d] = square(x)

        def arrive(d):
            got_chunk(d, 0)
            got_chunk(d, 1)
            got_rows(peer(d)).wait_recv()
            use(d)

        def bias(d):
            return LOG2E * rows[peer(d)] - x_sq[d]

        got_chunk(0, 0)
        got_chunk(0, 1)
        to_mirror.start()
        send_pair_pot().start()
        got_rows(peer(0)).wait_recv()
        use(0)
        make_score(0, 0, 0)
        fold(0, (0,), (bias(0),), True)

        @pl.loop(1, h)
        def _(i):
            d = 2 * i
            for chunk in range(2):
                got_chunk(d, chunk)
                pass_chunk(d, chunk).start()
            got_rows(peer(d)).wait_recv()
            pass_rows(d).start()
            use(d)
            make_score(1, 0, d)
            fold(0, (1,), (bias(d),), False)

        arrive(1)
        make_score(2, 0, 1)
        fold(0, (2,), (bias(1),), False)

        send_pair(own, 1 - half, 0, 1, mirror).wait_recv()
        pass_on.start()
        as_target(1, pair[1 - half])
        for d in range(3):
            make_score(3 + d, 1, d)
        fold(1, (3, 4, 5), [bias(d) for d in range(3)], True)

        @pl.loop(2, h)
        def _(i):
            make_score(3, 1, 2 * i)
            fold(1, (3,), (bias(2 * i),), False)

        @pl.loop(1, h)
        def _(i):
            d = 2 * i + 1
            arrive(d)
            for acc in range(2):
                make_score(acc, acc, d)
            for acc in range(2):
                fold(acc, (acc,), (bias(d),), False)

        pout[half] = finish(0) + LOG2E * (pot[...] - offset) - square(own[...])
        send_pair_pot().wait_recv()
        pout[1 - half] = finish(1) + LOG2E * (pair_pot[...] - offset) - square(pair[1 - half])
        pl.semaphore_wait(ready, n)
        sends = (send_e1(0, 3, mirror), send_e1(1, 1, mirror), send_e1(2, 3, cell))
        for copy in sends:
            copy.start()

        for slot, x in ((half, own[...]), (1 - half, pair[1 - half])):
            as_source(slot, x)
            pair_sq[slot] = square(x)

        for d in range(h):
            who = lax.rem(peer(d) + g, n)
            got_block(who).wait_recv()
            got_rows(who).wait_recv()
            x = block[who]
            as_target(d, x)
            x_sq[d] = square(x)
            for s in range(2):
                make_score(2 * d + s, d, s)

        got_e1(1 - half).wait_recv()
        joined = [join([pout[s], e1[1 - half, s]]) for s in range(2)]
        message(0, h, [joined[s] - pair_sq[s] for s in range(2)])

        @pl.loop(0, n)
        def _(i):
            send_parts(0, n - 1 - i).start()

        out_ref[...] = LN2 * join([pout[half], e1[1 - half, half]])
        for copy in (to_mirror, to_last, pass_on, send_pair_pot(), *sends):
            copy.wait_send()

        @pl.loop(1, h)
        def _(i):
            for chunk in range(2):
                pass_chunk(2 * i, chunk).wait_send()
            pass_rows(2 * i).wait_send()

        @pl.loop(0, n)
        def _(d):
            send_parts(0, d).wait_send()

    @pl.when(t == 2)
    def _():
        for d in range(g):
            if d < h:
                send_early(d).start()
                send_rows_early(d).start()
            else:
                send_rows(d, 3).start()
            send_block(d, 3).start()
            if d == 0:
                mirror_block().start()
        for d in range(g):
            if d < h:
                send_early(d).wait_send()
                send_rows_early(d).wait_send()
            else:
                send_rows(d, 3).wait_send()
            send_block(d, 3).wait_send()
        mirror_block().wait_send()
        send_final().wait_recv()
        out_ref[...] = final[...]

    @pl.when(t == 3)
    def _():
        for d in range(n):
            pl.semaphore_signal(ready, inc=1, device_id=(1, xor(cell, d, n)), device_id_type=MESH)
        as_target(g, own[...])

        def arrive_pair(slot):
            send_pair(own, slot, 0, 1, mirror).wait_recv()
            x = pair[slot]
            as_source(slot, x)
            pair_sq[slot] = square(x)

        arrive_pair(half)

        @pl.loop(h, g)
        def _(d):
            who = peer(d)
            got_block(who).wait_recv()
            got_rows(who).wait_recv()
            x = block[who]
            as_target(d, x)
            x_sq[who] = square(x)
            make_score(2 * d + half, d, half)

        got_block(mirror).wait_recv()
        for d in range(1, g):
            relay(d).start()
        arrive_pair(1 - half)

        @pl.loop(h, g)
        def _(d):
            make_score(2 * d + 1 - half, d, 1 - half)

        def prepare(who, base):
            x = block[who]
            k = lax.rem(who, g)
            as_source(k, x)
            x_sq[who] = square(x)
            make_score(base + k, g, k)

        @pl.loop(0, h)
        def _(d):
            got_block(peer(d)).wait_recv()
            prepare(peer(d), 0)

        @pl.loop(h, g)
        def _(d):
            prepare(peer(d), 0)

        for s in range(2):
            got_e1(s).wait_recv()
        biases = [join([e1[0, s], e1[1, s]]) - pair_sq[s] for s in range(2)]

        message(h, g, biases)

        @pl.loop(0, n - 1)
        def _(i):
            send_parts(1, n - 1 - i).start()

        prepare(mirror, g)

        @pl.loop(1, g)
        def _(d):
            who = lax.rem(peer(d) + g, n)
            got_block(who).wait_recv()
            prepare(who, g)

        def gather(start, skip):
            @pl.loop(0, g)
            def _(m):
                got_parts(0, start + m).wait_recv()

            @pl.loop(skip, g)
            def _(d):
                who = lax.rem(peer(d) + g, n) if skip == 0 else peer(d)
                got_parts(1, who).wait_recv()

            @pl.loop(0, g, unroll=BATCH)
            def _(k):
                beliefs[k] = join([parts[start + m, xor(k, m, g)] for m in range(g)])

            def fold_batch(first, size, begin):
                batch = [first + i for i in range(size)]
                fold(
                    0,
                    [(0 if skip == 1 else g) + m for m in batch],
                    [beliefs[m] - x_sq[start + m] for m in batch],
                    begin,
                )

            fold_batch(0, min(BATCH, g), skip == 1)

            @pl.loop(1, g // BATCH)
            def _(i):
                fold_batch(i * BATCH, BATCH, False)

        gather(first_cell, 1)
        final[...] = LN2 * beliefs[cell - first_cell]
        send_final().start()
        gather(n - g - first_cell, 0)
        out_ref[...] = LN2 * (finish(0) - square(own[...])) - offset + pot[...]

        for d in range(1, g):
            relay(d).wait_send()

        @pl.loop(1, n)
        def _(d):
            send_parts(1, d).wait_send()

        send_final().wait_send()


def body(n, coords, potentials):
    _, dim, local = coords.shape
    g = n // 2
    f32, bf16 = jnp.float32, jnp.bfloat16
    dma = pltpu.SemaphoreType.DMA
    row = (1, local)
    return pl.pallas_call(
        functools.partial(kernel, n),
        out_shape=pltpu.VMEM((1, local), f32),
        in_specs=[pl.BlockSpec(memory_space=pl.ANY)] * 2,
        out_specs=pl.BlockSpec(memory_space=pltpu.VMEM),
        scratch_shapes=[
            pltpu.VMEM((dim, local), f32),
            pltpu.VMEM(row, f32),
            pltpu.VMEM((2, dim, local), f32),
            pltpu.VMEM(row, f32),
            pltpu.VMEM((n, dim, local), f32),
            pltpu.VMEM((n, *row), f32),
            pltpu.VMEM((g + 1, local, 4 * dim), bf16),
            pltpu.VMEM((g, 4 * dim, local), bf16),
            pltpu.VMEM((n, local, local), f32),
            pltpu.VMEM((n, *row), f32),
            pltpu.VMEM((2, *row), f32),
            pltpu.VMEM((2, local, 128), f32),
            pltpu.VMEM((2, local, 128), f32),
            pltpu.VMEM((2, *row), f32),
            pltpu.VMEM((2, 2, *row), f32),
            pltpu.VMEM((n, g, *row), f32),
            pltpu.VMEM((g, *row), f32),
            pltpu.VMEM(row, f32),
            dma((2,)),
            dma((g,)),
            dma((g, 2)),
            dma((g // 2,)),
            dma((2,)),
            dma((g,)),
            dma((g,)),
            dma((3,)),
            dma((3,)),
            dma((n,)),
            dma,
            dma((n,)),
            dma((n, 2)),
            dma((n,)),
            dma((2,)),
            dma,
            dma((2,)),
            dma((2, n)),
            dma,
            pltpu.SemaphoreType.REGULAR,
        ],
        compiler_params=pltpu.CompilerParams(
            collective_id=0, has_side_effects=True, vmem_limit_bytes=60 * 1024 * 1024
        ),
        name="sweep",
    )(coords, potentials)


def solution(mesh):
    return jax.shard_map(
        functools.partial(body, mesh.shape["cell"]),
        mesh=mesh,
        in_specs=(P("tm", None, "cell"), P("tm", "cell")),
        out_specs=P("tm", "cell"),
        check_vma=False,
    )
```

```python
import functools
import math

import jax
import jax.numpy as jnp
from jax import lax
from jax.experimental import pallas as pl
from jax.experimental.pallas import tpu as pltpu
from jax.sharding import PartitionSpec as P

LOG2E = math.log2(math.e)
LN2 = math.log(2.0)
BATCH = 4
MESH = pl.DeviceIdType.MESH


def xor(a, b, size):
    out, bit = 0, 1
    while bit < size:
        out = out + bit * ((a // bit + b // bit) % 2)
        bit *= 2
    return out


def kernel(
    n,
    coords_hbm,
    pot_hbm,
    out_ref,
    own,
    pot,
    pair,
    pair_pot,
    block,
    rows,
    split_y,
    split_x,
    score,
    x_sq,
    pair_sq,
    top,
    total,
    pout,
    e1,
    parts,
    beliefs,
    final,
    load_sem,
    block_send,
    chunk_send,
    early_send,
    mirror_send,
    rows_send,
    relay_send,
    pair_send,
    e1_send,
    parts_send,
    final_send,
    block_recv,
    chunk_recv,
    rows_recv,
    pair_recv,
    pair_pot_recv,
    e1_recv,
    parts_recv,
    final_recv,
    ready,
):
    dim, local = own.shape
    g = n // 2
    h = g // 2
    offset = math.log(n * local)
    t = lax.axis_index("tm")
    cell = lax.axis_index("cell")
    half = cell // g
    mirror = lax.rem(cell + g, n)
    first_cell = half * g

    def peer(d):
        return first_cell + xor(cell - first_cell, d, g)

    direct = [*range(2, g, 2), 1, 0]

    barrier = pltpu.get_barrier_semaphore()

    def greet(group, who):
        pl.semaphore_signal(barrier, inc=1, device_id=(group, who), device_id_type=MESH)

    def remote(src, dst, send, recv, group, who):
        return pltpu.make_async_remote_copy(
            src_ref=src,
            dst_ref=dst,
            send_sem=send,
            recv_sem=recv,
            device_id=(group, who),
            device_id_type=MESH,
        )

    def send_chunk(d, chunk):
        part = pl.ds(chunk * (dim // 2), dim // 2)
        return remote(
            own.at[part], block.at[cell, part], chunk_send.at[d, chunk], chunk_recv.at[cell, chunk], 1, peer(d)
        )

    def pass_chunk(d, chunk):
        ref = block.at[peer(d), pl.ds(chunk * (dim // 2), dim // 2)]
        return remote(ref, ref, chunk_send.at[d, chunk], chunk_recv.at[peer(d), chunk], 1, peer(1))

    def pass_rows(d):
        ref = rows.at[peer(d)]
        return remote(ref, ref, rows_send.at[d], rows_recv.at[peer(d)], 1, peer(1))

    def send_block(d, group):
        return remote(own, block.at[cell], block_send.at[d], block_recv.at[cell], group, peer(d))

    def send_rows(d, group):
        return remote(pot, rows.at[cell], rows_send.at[d], rows_recv.at[cell], group, peer(d))

    def got_block(who):
        return remote(own, block.at[who], block_send.at[0], block_recv.at[who], t, mirror)

    def got_rows(who):
        return remote(pot, rows.at[who], rows_send.at[0], rows_recv.at[who], t, mirror)

    def send_pair(src, slot, index, group, who):
        return remote(src, pair.at[slot], pair_send.at[index], pair_recv.at[slot], group, who)

    def send_pair_pot():
        return remote(pot, pair_pot, mirror_send.at[1], pair_pot_recv, 1, mirror)

    def send_e1(index, group, who):
        return remote(pout, e1.at[half], e1_send.at[index], e1_recv.at[half], group, who)

    def got_e1(slot):
        return remote(pout, e1.at[slot], e1_send.at[0], e1_recv.at[slot], t, mirror)

    def mirror_block():
        return remote(own, block.at[cell], mirror_send.at[0], block_recv.at[cell], 3, mirror)

    def relay(d):
        return remote(
            block.at[mirror], block.at[mirror], relay_send.at[d], block_recv.at[mirror], 3, peer(d)
        )

    def parts_copy(side, owner, d, who):
        ref = parts.at[owner, pl.ds(side * h, g - h if side else h)]
        return remote(ref, ref, parts_send.at[d], parts_recv.at[side, owner], 3, who)

    def send_parts(side, d):
        return parts_copy(side, cell, d, xor(cell, d, n))

    def got_parts(side, owner):
        return parts_copy(side, owner, 0, mirror)

    def send_early(d):
        return remote(own, block.at[mirror], early_send.at[d], block_recv.at[mirror], 1, peer(d))

    def send_rows_early(d):
        return remote(pot, rows.at[mirror], rows_send.at[d], rows_recv.at[mirror], 1, peer(d))

    def send_final():
        return remote(final, final, final_send, final_recv, 2, cell)

    @pl.when(t == 1)
    def _():
        for d in direct:
            greet(0, peer(d))
        greet(1, peer(1))
        greet(1, mirror)
        for d in range(h):
            greet(2, peer(d))
        for d in range(n):
            greet(3, xor(cell, d, n))

    @pl.when(t == 2)
    def _():
        greet(3, cell)

    @pl.when(t == 3)
    def _():
        greet(1, cell)
        greet(2, mirror)
        for d in range(g):
            greet(2, peer(d))
        for d in range(1, n):
            greet(3, xor(cell, d, n))

    load_own = pltpu.make_async_copy(coords_hbm.at[0], own, load_sem.at[0])
    load_pot = pltpu.make_async_copy(pot_hbm, pot, load_sem.at[1])
    load_own.start()
    load_pot.start()
    load_own.wait()
    load_pot.wait()
    partners = jnp.where(t == 0, len(direct), jnp.where(t == 1, 3, jnp.where(t == 2, g + 1 + h, 2 * n)))
    pl.semaphore_wait(barrier, partners)

    def split(x):
        hi = x.astype(jnp.bfloat16)
        return hi, (x - hi.astype(jnp.float32)).astype(jnp.bfloat16)

    def as_target(slot, x):
        hi, lo = split((x * (2.0 * LOG2E)).T)
        split_y[slot, :, 0:dim] = hi
        split_y[slot, :, dim : 2 * dim] = hi
        split_y[slot, :, 2 * dim : 3 * dim] = lo
        split_y[slot, :, 3 * dim : 4 * dim] = lo

    def as_source(slot, x):
        hi, lo = split(x)
        split_x[slot, pl.ds(0, dim)] = hi
        split_x[slot, pl.ds(dim, dim)] = lo
        split_x[slot, pl.ds(2 * dim, dim)] = hi
        split_x[slot, pl.ds(3 * dim, dim)] = lo

    def square(x):
        return LOG2E * jnp.sum(x * x, axis=0, keepdims=True)

    def make_score(slot, target, source):
        score[slot] = lax.dot_general(
            split_y[target],
            split_x[source],
            (((1,), (0,)), ((), ())),
            preferred_element_type=jnp.float32,
        )

    def tree(op, values):
        while len(values) > 1:
            values = [op(*values[i : i + 2]) if i + 1 < len(values) else values[i] for i in range(0, len(values), 2)]
        return values[0]

    def fold(acc, slots, biases, first):
        size = 32 if len(slots) == 1 else 8
        for start in range(0, local, size):
            here = pl.ds(start, size)
            terms = [
                score[slot, here, pl.ds(k, 128)] + bias[:, k : k + 128]
                for slot, bias in zip(slots, biases)
                for k in range(0, local, 128)
            ]
            new = tree(jnp.maximum, terms)
            if not first:
                old = top[acc, here]
                new = jnp.maximum(old, new)
            mass = tree(jnp.add, [jnp.exp2(term - new) for term in terms])
            if not first:
                mass = mass + total[acc, here] * jnp.exp2(old - new)
            top[acc, here] = new
            total[acc, here] = mass

    def finish(acc):
        tops = top[acc].T
        peak = jnp.max(tops, axis=0, keepdims=True)
        mass = jnp.sum(total[acc].T * jnp.exp2(tops - peak), axis=0, keepdims=True)
        return peak + jnp.log2(mass)

    def join(values):
        peak = tree(jnp.maximum, values)
        return peak + jnp.log2(tree(jnp.add, [jnp.exp2(value - peak) for value in values]))

    def message(begin, end, biases):
        @pl.loop(begin // 2, end // 2)
        def _(i):
            for acc in range(2):
                d = 2 * i + acc
                fold(acc, (2 * d, 2 * d + 1), biases, True)
            for acc in range(2):
                d = 2 * i + acc
                who = lax.rem(peer(d) + g, n) if begin == 0 else peer(d)
                square_of = x_sq[d] if begin == 0 else x_sq[who]
                parts[cell, d] = finish(acc) + LOG2E * (rows[who] - offset) - square_of

    @pl.when(t == 0)
    def _():
        for d in direct:
            send_chunk(d, 0).start()
            send_rows(d, 1).start()
            send_chunk(d, 1).start()
        out_ref[...] = pot[...]
        for d in direct:
            for chunk in range(2):
                send_chunk(d, chunk).wait_send()
            send_rows(d, 1).wait_send()

    @pl.when(t == 1)
    def _():
        to_mirror = send_pair(own, half, 0, 1, mirror)
        to_last = send_pair(own, half, 1, 3, cell)
        pass_on = send_pair(pair.at[1 - half], 1 - half, 2, 3, cell)
        to_last.start()
        as_target(0, own[...])

        def got_chunk(d, chunk):
            return pass_chunk(d, chunk).wait_recv()

        def use(d):
            x = block[peer(d)]
            as_source(d, x)
            x_sq[d] = square(x)

        def arrive(d):
            got_chunk(d, 0)
            got_chunk(d, 1)
            got_rows(peer(d)).wait_recv()
            use(d)

        def bias(d):
            return LOG2E * rows[peer(d)] - x_sq[d]

        got_chunk(0, 0)
        got_chunk(0, 1)
        to_mirror.start()
        send_pair_pot().start()
        got_rows(peer(0)).wait_recv()
        use(0)
        make_score(0, 0, 0)
        fold(0, (0,), (bias(0),), True)

        @pl.loop(1, h)
        def _(i):
            d = 2 * i
            for chunk in range(2):
                got_chunk(d, chunk)
                pass_chunk(d, chunk).start()
            got_rows(peer(d)).wait_recv()
            pass_rows(d).start()
            use(d)
            make_score(1, 0, d)
            fold(0, (1,), (bias(d),), False)

        arrive(1)
        make_score(2, 0, 1)
        fold(0, (2,), (bias(1),), False)

        send_pair(own, 1 - half, 0, 1, mirror).wait_recv()
        pass_on.start()
        as_target(1, pair[1 - half])
        for d in range(3):
            make_score(3 + d, 1, d)
        fold(1, (3, 4, 5), [bias(d) for d in range(3)], True)

        @pl.loop(2, h)
        def _(i):
            make_score(3, 1, 2 * i)
            fold(1, (3,), (bias(2 * i),), False)

        @pl.loop(1, h)
        def _(i):
            d = 2 * i + 1
            arrive(d)
            for acc in range(2):
                make_score(acc, acc, d)
            for acc in range(2):
                fold(acc, (acc,), (bias(d),), False)

        pout[half] = finish(0) + LOG2E * (pot[...] - offset) - square(own[...])
        send_pair_pot().wait_recv()
        pout[1 - half] = finish(1) + LOG2E * (pair_pot[...] - offset) - square(pair[1 - half])
        pl.semaphore_wait(ready, n)
        sends = (send_e1(0, 3, mirror), send_e1(1, 1, mirror), send_e1(2, 3, cell))
        for copy in sends:
            copy.start()

        for slot, x in ((half, own[...]), (1 - half, pair[1 - half])):
            as_source(slot, x)
            pair_sq[slot] = square(x)

        for d in range(h):
            who = lax.rem(peer(d) + g, n)
            got_block(who).wait_recv()
            got_rows(who).wait_recv()
            x = block[who]
            as_target(d, x)
            x_sq[d] = square(x)
            for s in range(2):
                make_score(2 * d + s, d, s)

        got_e1(1 - half).wait_recv()
        joined = [join([pout[s], e1[1 - half, s]]) for s in range(2)]
        message(0, h, [joined[s] - pair_sq[s] for s in range(2)])

        @pl.loop(0, n)
        def _(i):
            send_parts(0, n - 1 - i).start()

        out_ref[...] = LN2 * join([pout[half], e1[1 - half, half]])
        for copy in (to_mirror, to_last, pass_on, send_pair_pot(), *sends):
            copy.wait_send()

        @pl.loop(1, h)
        def _(i):
            for chunk in range(2):
                pass_chunk(2 * i, chunk).wait_send()
            pass_rows(2 * i).wait_send()

        @pl.loop(0, n)
        def _(d):
            send_parts(0, d).wait_send()

    @pl.when(t == 2)
    def _():
        for d in range(g):
            if d < h:
                send_early(d).start()
                send_rows_early(d).start()
            else:
                send_rows(d, 3).start()
            send_block(d, 3).start()
            if d == 0:
                mirror_block().start()
        for d in range(g):
            if d < h:
                send_early(d).wait_send()
                send_rows_early(d).wait_send()
            else:
                send_rows(d, 3).wait_send()
            send_block(d, 3).wait_send()
        mirror_block().wait_send()
        send_final().wait_recv()
        out_ref[...] = final[...]

    @pl.when(t == 3)
    def _():
        for d in range(n):
            pl.semaphore_signal(ready, inc=1, device_id=(1, xor(cell, d, n)), device_id_type=MESH)
        as_target(g, own[...])

        def arrive_pair(slot):
            send_pair(own, slot, 0, 1, mirror).wait_recv()
            x = pair[slot]
            as_source(slot, x)
            pair_sq[slot] = square(x)

        arrive_pair(half)

        @pl.loop(h, g)
        def _(d):
            who = peer(d)
            got_block(who).wait_recv()
            got_rows(who).wait_recv()
            x = block[who]
            as_target(d, x)
            x_sq[who] = square(x)
            make_score(2 * d + half, d, half)

        got_block(mirror).wait_recv()
        for d in range(1, g):
            relay(d).start()
        def prepare(who, base):
            x = block[who]
            k = lax.rem(who, g)
            as_source(k, x)
            x_sq[who] = square(x)
            make_score(base + k, g, k)

        @pl.loop(0, h)
        def _(d):
            got_block(peer(d)).wait_recv()
            prepare(peer(d), 0)

        @pl.loop(h, g)
        def _(d):
            prepare(peer(d), 0)

        arrive_pair(1 - half)

        @pl.loop(h, g)
        def _(d):
            make_score(2 * d + 1 - half, d, 1 - half)

        for s in range(2):
            got_e1(s).wait_recv()
        biases = [join([e1[0, s], e1[1, s]]) - pair_sq[s] for s in range(2)]

        message(h, g, biases)

        @pl.loop(0, n - 1)
        def _(i):
            send_parts(1, n - 1 - i).start()

        prepare(mirror, g)

        @pl.loop(1, g)
        def _(d):
            who = lax.rem(peer(d) + g, n)
            got_block(who).wait_recv()
            prepare(who, g)

        def gather(start, skip):
            @pl.loop(0, g)
            def _(m):
                got_parts(0, start + m).wait_recv()

            @pl.loop(skip, g)
            def _(d):
                who = lax.rem(peer(d) + g, n) if skip == 0 else peer(d)
                got_parts(1, who).wait_recv()

            @pl.loop(0, g, unroll=BATCH)
            def _(k):
                beliefs[k] = join([parts[start + m, xor(k, m, g)] for m in range(g)])

            def fold_batch(first, size, begin):
                batch = [first + i for i in range(size)]
                fold(
                    0,
                    [(0 if skip == 1 else g) + m for m in batch],
                    [beliefs[m] - x_sq[start + m] for m in batch],
                    begin,
                )

            fold_batch(0, min(BATCH, g), skip == 1)

            @pl.loop(1, g // BATCH)
            def _(i):
                fold_batch(i * BATCH, BATCH, False)

        gather(first_cell, 1)
        final[...] = LN2 * beliefs[cell - first_cell]
        send_final().start()
        gather(n - g - first_cell, 0)
        out_ref[...] = LN2 * (finish(0) - square(own[...])) - offset + pot[...]

        for d in range(1, g):
            relay(d).wait_send()

        @pl.loop(1, n)
        def _(d):
            send_parts(1, d).wait_send()

        send_final().wait_send()


def body(n, coords, potentials):
    _, dim, local = coords.shape
    g = n // 2
    f32, bf16 = jnp.float32, jnp.bfloat16
    dma = pltpu.SemaphoreType.DMA
    row = (1, local)
    return pl.pallas_call(
        functools.partial(kernel, n),
        out_shape=pltpu.VMEM((1, local), f32),
        in_specs=[pl.BlockSpec(memory_space=pl.ANY)] * 2,
        out_specs=pl.BlockSpec(memory_space=pltpu.VMEM),
        scratch_shapes=[
            pltpu.VMEM((dim, local), f32),
            pltpu.VMEM(row, f32),
            pltpu.VMEM((2, dim, local), f32),
            pltpu.VMEM(row, f32),
            pltpu.VMEM((n, dim, local), f32),
            pltpu.VMEM((n, *row), f32),
            pltpu.VMEM((g + 1, local, 4 * dim), bf16),
            pltpu.VMEM((g, 4 * dim, local), bf16),
            pltpu.VMEM((n, local, local), f32),
            pltpu.VMEM((n, *row), f32),
            pltpu.VMEM((2, *row), f32),
            pltpu.VMEM((2, local, 128), f32),
            pltpu.VMEM((2, local, 128), f32),
            pltpu.VMEM((2, *row), f32),
            pltpu.VMEM((2, 2, *row), f32),
            pltpu.VMEM((n, g, *row), f32),
            pltpu.VMEM((g, *row), f32),
            pltpu.VMEM(row, f32),
            dma((2,)),
            dma((g,)),
            dma((g, 2)),
            dma((g // 2,)),
            dma((2,)),
            dma((g,)),
            dma((g,)),
            dma((3,)),
            dma((3,)),
            dma((n,)),
            dma,
            dma((n,)),
            dma((n, 2)),
            dma((n,)),
            dma((2,)),
            dma,
            dma((2,)),
            dma((2, n)),
            dma,
            pltpu.SemaphoreType.REGULAR,
        ],
        compiler_params=pltpu.CompilerParams(
            collective_id=0, has_side_effects=True, vmem_limit_bytes=60 * 1024 * 1024
        ),
        name="sweep",
    )(coords, potentials)


def solution(mesh):
    return jax.shard_map(
        functools.partial(body, mesh.shape["cell"]),
        mesh=mesh,
        in_specs=(P("tm", None, "cell"), P("tm", "cell")),
        out_specs=P("tm", "cell"),
        check_vma=False,
    )
```
